512 devices in a mesh: dp: 32 (over z, x_hi, core), fsdp: 16 (over x_lo, y).
Axes of the slice: x: 4 (x_hi: 2, x_lo: 2; x = x_hi * 2 + x_lo), y: 8, z: 8, core: 2. Of those that a mesh axis runs over, the one named last changes fastest.
Arguments:
- tokens: bfloat16 [5120, 4608], P('fsdp'), may hold values from -12 to 12
- cotangent: bfloat16 [5120, 12288], P('fsdp', 'dp'), may hold values from -0.046875 to 0.046875
- gain: float32 [4608], replicated, may hold values from 0.5 to 1.5
- master: float32 [4608, 12288], P('fsdp', 'dp'), may hold values from -0.09375 to 0.09375
- momentum: float32 [4608, 12288], P('fsdp', 'dp'), may hold values from -3 to 3
Outputs:
- new_master: float32 [4608, 12288], P('fsdp', 'dp')
- new_momentum: float32 [4608, 12288], P('fsdp', 'dp')
The draws below stay inside these ranges and needn't reach their ends.
All inputs are finite; a program needn't handle non-finite values.
Results may differ from the reference program's by a relative error of at most 0.0024.
Values may be sent and summed in bfloat16 or wider, within the bound.
A program may use at most 64 MiB of HBM per device.

```python
import math
import jax
import jax.numpy as jnp
from jax import lax

D = 4608
FF = 12288
TOK_DEV = 320
TOKENS = 5120
N_DP = 32
N_FSDP = 16


def shared_signs(key):
    sign_bits = jax.random.randint(jax.random.fold_in(key, 101), (TOKENS,), 0, 2)
    return (2 * sign_bits - 1).astype(jnp.float32)


def block_levels(key, block_count, block_width, spread):
    blocks = jnp.exp(jax.random.uniform(key, (block_count,), jnp.float32, -spread, spread))
    fine_key = jax.random.fold_in(key, 7)
    fine_part = jnp.exp(jax.random.uniform(fine_key, (block_count * block_width,), jnp.float32, -0.5, 0.5))
    return jnp.repeat(blocks, block_width) * fine_part


def draw_tokens(key, part):
    signs = shared_signs(key)
    levels = block_levels(jax.random.fold_in(key, 201), N_FSDP, D // N_FSDP, 1.2)
    noise_key = jax.random.fold_in(key, 202)
    common_key = jax.random.fold_in(key, 203)
    random_part = jax.random.truncated_normal(noise_key, -4.0, 4.0, (TOKENS, D), jnp.float32)
    common = jax.random.truncated_normal(common_key, -4.0, 4.0, (D,), jnp.float32)
    amount = 0.08
    row_scale = jnp.ones((TOKENS,), jnp.float32)
    values = row_scale[:, None] * levels[None, :] * (random_part + amount * signs[:, None] * common[None, :])
    return jnp.clip(values, -12.0, 12.0).astype(jnp.bfloat16)


def draw_cotangent(key, part):
    signs = shared_signs(key)
    col_levels = block_levels(jax.random.fold_in(key, 301), N_DP, FF // N_DP, 1.2)
    row_blocks = jnp.exp(jax.random.uniform(jax.random.fold_in(key, 302), (N_FSDP,), jnp.float32, -0.8, 0.8))
    row_levels = jnp.repeat(row_blocks, TOK_DEV)
    noise_key = jax.random.fold_in(key, 303)
    common_key = jax.random.fold_in(key, 304)
    random_part = jax.random.truncated_normal(noise_key, -4.0, 4.0, (TOKENS, FF), jnp.float32)
    common = jax.random.truncated_normal(common_key, -4.0, 4.0, (FF,), jnp.float32)
    size_factor = 14.0
    values = size_factor / TOKENS * row_levels[:, None] * col_levels[None, :] * (random_part + signs[:, None] * common[None, :])
    limit = 240.0 / TOKENS
    return jnp.clip(values, -limit, limit).astype(jnp.bfloat16)


def shard_levels(own_key, extent, cuts, smallest, largest):
    loudness, own = 1.0, jax.random.fold_in(own_key, 6)
    for axis_at, parts in cuts:
        heights = jnp.exp(jax.random.uniform(jax.random.fold_in(own, axis_at), (parts,), jnp.float32, smallest / len(cuts), largest / len(cuts)))
        loudness = loudness * jnp.repeat(heights, extent[axis_at] // parts).reshape([-1 if axis == axis_at else 1 for axis in range(len(extent))])
    return loudness


def gaussian(own_key, shape, width, most, shards=(), held_as=jnp.bfloat16):
    array = width * jax.random.normal(own_key, shape, jnp.float32)
    if shards:
        array = array * shard_levels(own_key, shape, shards, -0.22, 0.18)
    return jnp.clip(array, -most, most).astype(held_as)


def setup_inputs(seed: int = 0) -> dict:
    splits = jax.random.split(jax.random.key(seed), 6)
    return {
        "tokens": draw_tokens(jax.random.fold_in(splits[5], 71), 0),
        "cotangent": draw_cotangent(jax.random.fold_in(splits[5], 71), 0),
        "gain": jnp.clip(1.0 + 0.1 * jax.random.normal(splits[2], (D,), jnp.float32), 0.5, 1.5),
        "master": gaussian(splits[3], (D, FF), D ** -0.5, 0.09375, ((0, 16), (1, 32)), jnp.float32),
        "momentum": gaussian(splits[4], (D, FF), 0.5, 3.0, ((0, 16), (1, 32)), jnp.float32),
    }


inv_root_two = 1.0 / math.sqrt(2.0)
inv_root_two_pi = 1.0 / math.sqrt(2.0 * math.pi)

def norm_rows(tokens, gain):
    values = tokens.astype(jnp.float32)
    meansq = lax.optimization_barrier(jnp.mean(values * values, axis=1, keepdims=True))
    return (values * lax.rsqrt(meansq + 1e-06) * gain).astype(jnp.bfloat16)

def slope_of(pre):
    cdf = 0.5 * (1.0 + jax.scipy.special.erf(pre * inv_root_two))
    return cdf + pre * jnp.exp(-0.5 * pre * pre) * inv_root_two_pi

def summed(normed, cotangent, weights):
    pre = jnp.dot(normed, weights, preferred_element_type=jnp.float32)
    dpre = (cotangent.astype(jnp.float32) * slope_of(pre)).astype(jnp.bfloat16)
    norm_blocks = normed.reshape(N_FSDP, TOK_DEV, D)
    dpre_blocks = dpre.reshape(N_FSDP, TOK_DEV, FF)
    dims = (((0,), (0,)), ((), ()))

    def add_block(total, pair):
        term = lax.dot_general(pair[0], pair[1], dims, preferred_element_type=jnp.float32).astype(jnp.bfloat16)
        term = lax.optimization_barrier(term)
        return (total + term.astype(jnp.float32), None)
    total, unused = lax.scan(add_block, jnp.zeros((D, FF), jnp.float32), (norm_blocks, dpre_blocks))
    return total

def reference(tokens, cotangent, gain, master, momentum):
    normed = norm_rows(tokens, gain)
    first = summed(normed, cotangent, master.astype(jnp.bfloat16))
    scale = math.sqrt(FF) / 4.0 / (jnp.sqrt(jnp.sum(first * first)) + 1e-12)
    perturbed = (master + scale * first).astype(jnp.bfloat16)
    second = summed(normed, cotangent, perturbed)
    new_momentum = 0.9 * momentum + second
    new_master = master - 0.002 * new_momentum
    return (new_master, new_momentum)
```

```python
import math

import jax
import jax.numpy as jnp
from jax import lax
from jax.sharding import PartitionSpec as P

FF = 12288


inv_root_two = 1.0 / math.sqrt(2.0)
inv_root_two_pi = 1.0 / math.sqrt(2.0 * math.pi)


def norm_rows(tokens, gain):
    values = tokens.astype(jnp.float32)
    meansq = jnp.mean(values * values, axis=1, keepdims=True)
    return (values * lax.rsqrt(meansq + 1e-06) * gain).astype(jnp.bfloat16)


def slope_of(pre):
    cdf = 0.5 * (1.0 + jax.scipy.special.erf(pre * inv_root_two))
    return cdf + pre * jnp.exp(-0.5 * pre * pre) * inv_root_two_pi


def local(tokens, cotangent, gain, master, momentum):
    own_rows = master.shape[0]
    own_tokens = tokens.shape[0]
    n_shard = lax.axis_size("fsdp")
    n_copy = lax.axis_size("dp")
    share = own_tokens // n_copy
    along_rows = (((0,), (0,)), ((), ()))
    along_features = (((1,), (1,)), ((), ()))
    cot = cotangent.astype(jnp.float32)

    normed = norm_rows(tokens, gain)
    weights = lax.all_gather(master.astype(jnp.bfloat16), "fsdp", axis=0, tiled=True)
    mine = lax.dynamic_slice_in_dim(normed, lax.axis_index("dp") * share, share, 0)
    some = lax.all_gather(mine, "fsdp", axis=0, tiled=True)
    gram = lax.dot_general(
        some, normed, along_features, preferred_element_type=jnp.float32
    ).astype(jnp.bfloat16)
    columns = lax.dynamic_slice_in_dim(some, lax.axis_index("fsdp") * own_rows, own_rows, 1)
    both = lax.all_gather(jnp.concatenate([gram, columns], axis=1), "dp", axis=0, tiled=True)
    both = both.reshape(n_copy, n_shard, share, own_tokens + own_rows)
    both = both.transpose(1, 0, 2, 3).reshape(n_shard * own_tokens, own_tokens + own_rows)
    gram_all = both[:, :own_tokens]
    columns_all = both[:, own_tokens:]

    def gathered(pre):
        dpre = (cot * slope_of(pre)).astype(jnp.bfloat16)
        return dpre, lax.all_gather(dpre, "fsdp", axis=0, tiled=True)

    pre = jnp.dot(normed, weights, preferred_element_type=jnp.float32)
    dpre, dpre_all = gathered(pre)
    shift = lax.dot_general(gram_all, dpre_all, along_rows, preferred_element_type=jnp.float32)
    squares = lax.psum(jnp.sum(dpre.astype(jnp.float32) * shift), ("dp", "fsdp"))
    scale = math.sqrt(FF) / 4.0 / (jnp.sqrt(jnp.maximum(squares, 0.0)) + 1e-12)
    unused, dpre_two = gathered(pre + scale * shift)
    second = lax.dot_general(columns_all, dpre_two, along_rows, preferred_element_type=jnp.float32)
    new_momentum = 0.9 * momentum + second
    new_master = master - 0.002 * new_momentum
    return (new_master, new_momentum)


def solution(mesh):
    in_specs = (P("fsdp", None), P("fsdp", "dp"), P(), P("fsdp", "dp"), P("fsdp", "dp"))
    out_specs = (P("fsdp", "dp"), P("fsdp", "dp"))
    return jax.shard_map(local, mesh=mesh, in_specs=in_specs, out_specs=out_specs, check_vma=False)
```

```python
import functools
import math

import jax
import jax.numpy as jnp
from jax import lax
from jax.experimental import pallas as pl
from jax.experimental.pallas import tpu as pltpu
from jax.sharding import PartitionSpec as P

FF = 12288


inv_root_two = 1.0 / math.sqrt(2.0)
inv_root_two_pi = 1.0 / math.sqrt(2.0 * math.pi)


def norm_rows(tokens, gain):
    values = tokens.astype(jnp.float32)
    meansq = jnp.mean(values * values, axis=1, keepdims=True)
    return (values * lax.rsqrt(meansq + 1e-06) * gain).astype(jnp.bfloat16)


def slope_of(pre):
    cdf = 0.5 * (1.0 + jax.scipy.special.erf(pre * inv_root_two))
    return cdf + pre * jnp.exp(-0.5 * pre * pre) * inv_root_two_pi


RING = 8
MESH = pl.DeviceIdType.MESH


def gather_kernel(cut, x_ref, o_ref, side_send, side_recv, ring_send, ring_recv, local_sem):
    me = lax.axis_index("fsdp")
    column = lax.div(me, RING)
    row = lax.rem(me, RING)
    other = 1 - column
    side = other * RING + row
    ring = (
        column * RING + lax.rem(row + 1, RING),
        column * RING + lax.rem(row + RING - 1, RING),
    )
    total = x_ref.shape[0]
    part = (pl.ds(0, cut), pl.ds(cut, total - cut))

    barrier = pltpu.get_barrier_semaphore()
    for peer in (side, ring[0], ring[1]):
        pl.semaphore_signal(barrier, inc=1, device_id={"fsdp": peer}, device_id_type=MESH)
    pl.semaphore_wait(barrier, 3)

    own = pltpu.make_async_copy(x_ref, o_ref.at[me], local_sem)
    own.start()

    started = []

    def move(src, dst, send, recv, peer):
        return pltpu.make_async_remote_copy(
            src_ref=src,
            dst_ref=dst,
            send_sem=send,
            recv_sem=recv,
            device_id={"fsdp": peer},
            device_id_type=MESH,
        )

    def to_side(slot, origin, half, src=None):
        place = o_ref.at[origin, part[half]]
        copy = move(
            place if src is None else src, place, side_send.at[slot], side_recv.at[slot], side
        )
        copy.start()
        started.append(copy)

    def to_ring(unit, way, hop, origin, half, src=None):
        place = o_ref.at[origin, part[half]]
        at = (unit * 2 + way) * 4 + hop - 1
        copy = move(
            place if src is None else src, place, ring_send.at[at], ring_recv.at[at], ring[way]
        )
        copy.start()
        started.append(copy)

    hops = ((4, 3), (3, 4), (4, 3))
    halves = (0, 1, 1)
    columns = (column, column, other)

    first, second = x_ref.at[part[0]], x_ref.at[part[1]]
    to_side(0, me, 1, second)
    for way in range(2):
        to_ring(1, way, 1, me, 1, second)
    for way in range(2):
        to_ring(0, way, 1, me, 0, first)
    to_side(1, me, 0, first)
    place = o_ref.at[side, part[1]]
    move(place, place, side_send.at[0], side_recv.at[0], side).wait_recv()
    for way in range(2):
        to_ring(2, way, 1, side, 1)
    for hop in range(1, 5):
        for unit in (1, 0, 2):
            for way in range(2):
                if hop > hops[unit][way]:
                    continue
                source = lax.rem(row + (RING - hop if way == 0 else hop), RING)
                origin = columns[unit] * RING + source
                place = o_ref.at[origin, part[halves[unit]]]
                at = (unit * 2 + way) * 4 + hop - 1
                move(place, place, ring_send.at[at], ring_recv.at[at], ring[way]).wait_recv()
                if hop < hops[unit][way]:
                    to_ring(unit, way, hop + 1, origin, halves[unit])
                if unit == 0:
                    to_side(2 + way * 4 + hop - 1, origin, 0)
    place = o_ref.at[side, part[0]]
    move(place, place, side_send.at[1], side_recv.at[1], side).wait_recv()
    for way in range(2):
        for hop in range(1, hops[0][way] + 1):
            source = lax.rem(row + (RING - hop if way == 0 else hop), RING)
            place = o_ref.at[other * RING + source, part[0]]
            slot = 2 + way * 4 + hop - 1
            move(place, place, side_send.at[slot], side_recv.at[slot], side).wait_recv()
    for copy in started:
        copy.wait_send()
    own.wait()


def gather_rows(block, call):
    total, width = block.shape
    n_shard = lax.axis_size("fsdp")
    whole = pl.pallas_call(
        functools.partial(gather_kernel, total // 32 * 16),
        out_shape=jax.ShapeDtypeStruct((n_shard, total, width), block.dtype),
        in_specs=[pl.BlockSpec(memory_space=pltpu.VMEM)],
        out_specs=pl.BlockSpec(memory_space=pltpu.VMEM),
        scratch_shapes=[
            pltpu.SemaphoreType.DMA((10,)),
            pltpu.SemaphoreType.DMA((10,)),
            pltpu.SemaphoreType.DMA((24,)),
            pltpu.SemaphoreType.DMA((24,)),
            pltpu.SemaphoreType.DMA,
        ],
        compiler_params=pltpu.CompilerParams(collective_id=call, has_side_effects=True),
        cost_estimate=pl.CostEstimate(
            flops=0, bytes_accessed=30 * n_shard * total * width, transcendentals=0
        ),
    )(block)
    return whole.reshape(n_shard * total, width)


def share_kernel(axis, count, x_ref, o_ref, slots, send, recv):
    me = lax.axis_index(axis)
    peers = [lax.rem(me + step, count) for step in range(1, count)]
    barrier = pltpu.get_barrier_semaphore()
    for peer in peers:
        pl.semaphore_signal(barrier, inc=1, device_id={axis: peer}, device_id_type=MESH)
    pl.semaphore_wait(barrier, count - 1)
    copies = []
    for at, peer in enumerate(peers):
        copy = pltpu.make_async_remote_copy(
            src_ref=x_ref,
            dst_ref=slots.at[at],
            send_sem=send.at[at],
            recv_sem=recv.at[at],
            device_id={axis: peer},
            device_id_type=MESH,
        )
        copy.start()
        copies.append(copy)
    for copy in copies:
        copy.wait()
    o_ref[...] = x_ref[...] + jnp.sum(slots[...], axis=0)


def summed_over(axis, tile, call):
    count = lax.axis_size(axis)
    return pl.pallas_call(
        functools.partial(share_kernel, axis, count),
        out_shape=jax.ShapeDtypeStruct(tile.shape, tile.dtype),
        in_specs=[pl.BlockSpec(memory_space=pltpu.VMEM)],
        out_specs=pl.BlockSpec(memory_space=pltpu.VMEM),
        scratch_shapes=[
            pltpu.VMEM((count - 1,) + tile.shape, tile.dtype),
            pltpu.SemaphoreType.DMA((count - 1,)),
            pltpu.SemaphoreType.DMA((count - 1,)),
        ],
        compiler_params=pltpu.CompilerParams(collective_id=call, has_side_effects=True),
    )(tile)


def local(tokens, cotangent, gain, master, momentum):
    own_rows = master.shape[0]
    own_tokens = tokens.shape[0]
    n_shard = lax.axis_size("fsdp")
    n_copy = lax.axis_size("dp")
    share = own_tokens // n_copy
    along_rows = (((0,), (0,)), ((), ()))
    along_features = (((1,), (1,)), ((), ()))
    cot = cotangent.astype(jnp.float32)

    normed = norm_rows(tokens, gain)
    mine = lax.dynamic_slice_in_dim(normed, lax.axis_index("dp") * share, share, 0)
    some = gather_rows(mine.reshape(-1, 128), 0).reshape(-1, normed.shape[1])
    gram = lax.dot_general(
        some, normed, along_features, preferred_element_type=jnp.float32
    ).astype(jnp.bfloat16)
    columns = lax.dynamic_slice_in_dim(some, lax.axis_index("fsdp") * own_rows, own_rows, 1)
    piece, rounded = lax.optimization_barrier(
        (jnp.concatenate([gram, columns], axis=1), master.astype(jnp.bfloat16))
    )
    both = lax.all_gather(piece, "dp", axis=0, tiled=True)
    weights = gather_rows(rounded, 1)
    both = both.reshape(n_copy, n_shard, share, own_tokens + own_rows)
    both = both.transpose(1, 0, 2, 3).reshape(n_shard * own_tokens, own_tokens + own_rows)
    gram_all = both[:, :own_tokens]
    columns_all = both[:, own_tokens:]

    def gathered(pre, call):
        dpre = (cot * slope_of(pre)).astype(jnp.bfloat16)
        return dpre, gather_rows(dpre, call)

    pre = jnp.dot(normed, weights, preferred_element_type=jnp.float32)
    dpre, dpre_all = gathered(pre, 2)
    shift = lax.dot_general(gram_all, dpre_all, along_rows, preferred_element_type=jnp.float32)
    products = (dpre.astype(jnp.float32) * shift).reshape(-1, 8, 128)
    partial = summed_over("fsdp", jnp.sum(products, axis=0), 4)
    squares = jnp.sum(summed_over("dp", partial, 5))
    scale = math.sqrt(FF) / 4.0 / (jnp.sqrt(jnp.maximum(squares, 0.0)) + 1e-12)
    unused, dpre_two = gathered(pre + scale * shift, 3)
    second = lax.dot_general(columns_all, dpre_two, along_rows, preferred_element_type=jnp.float32)
    new_momentum = 0.9 * momentum + second
    new_master = master - 0.002 * new_momentum
    return (new_master, new_momentum)


def solution(mesh):
    in_specs = (P("fsdp", None), P("fsdp", "dp"), P(), P("fsdp", "dp"), P("fsdp", "dp"))
    out_specs = (P("fsdp", "dp"), P("fsdp", "dp"))
    return jax.shard_map(local, mesh=mesh, in_specs=in_specs, out_specs=out_specs, check_vma=False)
```

```python
import functools
import math

import jax
import jax.numpy as jnp
from jax import lax
from jax.experimental import pallas as pl
from jax.experimental.pallas import tpu as pltpu
from jax.sharding import PartitionSpec as P

FF = 12288


inv_root_two = 1.0 / math.sqrt(2.0)
inv_root_two_pi = 1.0 / math.sqrt(2.0 * math.pi)


def norm_rows(tokens, gain):
    values = tokens.astype(jnp.float32)
    meansq = jnp.mean(values * values, axis=1, keepdims=True)
    return (values * lax.rsqrt(meansq + 1e-06) * gain).astype(jnp.bfloat16)


def slope_of(pre):
    cdf = 0.5 * (1.0 + jax.scipy.special.erf(pre * inv_root_two))
    return cdf + pre * jnp.exp(-0.5 * pre * pre) * inv_root_two_pi


RING = 8
MESH = pl.DeviceIdType.MESH


def gather_kernel(cut, x_ref, o_ref, side_send, side_recv, ring_send, ring_recv, local_sem):
    me = lax.axis_index("fsdp")
    column = lax.div(me, RING)
    row = lax.rem(me, RING)
    other = 1 - column
    side = other * RING + row
    ring = (
        column * RING + lax.rem(row + 1, RING),
        column * RING + lax.rem(row + RING - 1, RING),
    )
    total = x_ref.shape[0]
    part = (pl.ds(0, cut), pl.ds(cut, total - cut))

    barrier = pltpu.get_barrier_semaphore()
    for peer in (side, ring[0], ring[1]):
        pl.semaphore_signal(barrier, inc=1, device_id={"fsdp": peer}, device_id_type=MESH)
    pl.semaphore_wait(barrier, 3)

    own = pltpu.make_async_copy(x_ref, o_ref.at[me], local_sem)
    own.start()

    started = []

    def move(src, dst, send, recv, peer):
        return pltpu.make_async_remote_copy(
            src_ref=src,
            dst_ref=dst,
            send_sem=send,
            recv_sem=recv,
            device_id={"fsdp": peer},
            device_id_type=MESH,
        )

    def to_side(slot, origin, half, src=None):
        place = o_ref.at[origin, part[half]]
        copy = move(
            place if src is None else src, place, side_send.at[slot], side_recv.at[slot], side
        )
        copy.start()
        started.append(copy)

    def to_ring(unit, way, hop, origin, half, src=None):
        place = o_ref.at[origin, part[half]]
        at = (unit * 2 + way) * 4 + hop - 1
        copy = move(
            place if src is None else src, place, ring_send.at[at], ring_recv.at[at], ring[way]
        )
        copy.start()
        started.append(copy)

    hops = ((4, 3), (3, 4), (4, 3))
    halves = (0, 1, 1)
    columns = (column, column, other)

    first, second = x_ref.at[part[0]], x_ref.at[part[1]]
    to_side(0, me, 1, second)
    for way in range(2):
        to_ring(1, way, 1, me, 1, second)
    for way in range(2):
        to_ring(0, way, 1, me, 0, first)
    to_side(1, me, 0, first)
    place = o_ref.at[side, part[1]]
    move(place, place, side_send.at[0], side_recv.at[0], side).wait_recv()
    for way in range(2):
        to_ring(2, way, 1, side, 1)
    for hop in range(1, 5):
        for unit in (1, 0, 2):
            for way in range(2):
                if hop > hops[unit][way]:
                    continue
                source = lax.rem(row + (RING - hop if way == 0 else hop), RING)
                origin = columns[unit] * RING + source
                place = o_ref.at[origin, part[halves[unit]]]
                at = (unit * 2 + way) * 4 + hop - 1
                move(place, place, ring_send.at[at], ring_recv.at[at], ring[way]).wait_recv()
                if hop < hops[unit][way]:
                    to_ring(unit, way, hop + 1, origin, halves[unit])
                if unit == 0:
                    to_side(2 + way * 4 + hop - 1, origin, 0)
    place = o_ref.at[side, part[0]]
    move(place, place, side_send.at[1], side_recv.at[1], side).wait_recv()
    for way in range(2):
        for hop in range(1, hops[0][way] + 1):
            source = lax.rem(row + (RING - hop if way == 0 else hop), RING)
            place = o_ref.at[other * RING + source, part[0]]
            slot = 2 + way * 4 + hop - 1
            move(place, place, side_send.at[slot], side_recv.at[slot], side).wait_recv()
    for copy in started:
        copy.wait_send()
    own.wait()


def gather_rows(block, call):
    total, width = block.shape
    n_shard = lax.axis_size("fsdp")
    whole = pl.pallas_call(
        functools.partial(gather_kernel, total // 32 * 16),
        out_shape=jax.ShapeDtypeStruct((n_shard, total, width), block.dtype),
        in_specs=[pl.BlockSpec(memory_space=pltpu.VMEM)],
        out_specs=pl.BlockSpec(memory_space=pltpu.VMEM),
        scratch_shapes=[
            pltpu.SemaphoreType.DMA((10,)),
            pltpu.SemaphoreType.DMA((10,)),
            pltpu.SemaphoreType.DMA((24,)),
            pltpu.SemaphoreType.DMA((24,)),
            pltpu.SemaphoreType.DMA,
        ],
        compiler_params=pltpu.CompilerParams(collective_id=call, has_side_effects=True),
        cost_estimate=pl.CostEstimate(
            flops=0, bytes_accessed=30 * n_shard * total * width, transcendentals=0
        ),
    )(block)
    return whole.reshape(n_shard * total, width)


def share_kernel(axis, count, x_ref, o_ref, slots, send, recv):
    me = lax.axis_index(axis)
    peers = [lax.rem(me + step, count) for step in range(1, count)]
    barrier = pltpu.get_barrier_semaphore()
    for peer in peers:
        pl.semaphore_signal(barrier, inc=1, device_id={axis: peer}, device_id_type=MESH)
    pl.semaphore_wait(barrier, count - 1)
    copies = []
    for at, peer in enumerate(peers):
        copy = pltpu.make_async_remote_copy(
            src_ref=x_ref,
            dst_ref=slots.at[at],
            send_sem=send.at[at],
            recv_sem=recv.at[at],
            device_id={axis: peer},
            device_id_type=MESH,
        )
        copy.start()
        copies.append(copy)
    for copy in copies:
        copy.wait()
    o_ref[...] = x_ref[...] + jnp.sum(slots[...], axis=0)


def summed_over(axis, tile, call):
    count = lax.axis_size(axis)
    return pl.pallas_call(
        functools.partial(share_kernel, axis, count),
        out_shape=jax.ShapeDtypeStruct(tile.shape, tile.dtype),
        in_specs=[pl.BlockSpec(memory_space=pltpu.VMEM)],
        out_specs=pl.BlockSpec(memory_space=pltpu.VMEM),
        scratch_shapes=[
            pltpu.VMEM((count - 1,) + tile.shape, tile.dtype),
            pltpu.SemaphoreType.DMA((count - 1,)),
            pltpu.SemaphoreType.DMA((count - 1,)),
        ],
        compiler_params=pltpu.CompilerParams(collective_id=call, has_side_effects=True),
    )(tile)


def local(tokens, cotangent, gain, master, momentum):
    own_rows = master.shape[0]
    own_tokens = tokens.shape[0]
    n_shard = lax.axis_size("fsdp")
    n_copy = lax.axis_size("dp")
    share = own_tokens // n_copy
    along_rows = (((0,), (0,)), ((), ()))
    along_features = (((1,), (1,)), ((), ()))
    cot = cotangent.astype(jnp.float32)

    normed = norm_rows(tokens, gain)
    tall = share // 8 * 8
    short = share - tall
    position = lax.axis_index("dp")
    mine = jnp.concatenate(
        [
            lax.dynamic_slice_in_dim(normed, position * tall, tall, 0),
            lax.dynamic_slice_in_dim(normed, n_copy * tall + position * short, short, 0),
        ]
    )
    some = gather_rows(mine.reshape(-1, 128), 0).reshape(n_shard, share, -1)
    some = jnp.concatenate(
        [
            some[:, :tall].reshape(n_shard * tall, -1),
            some[:, tall:].reshape(n_shard * short, -1),
        ]
    )
    gram = lax.dot_general(
        some, normed, along_features, preferred_element_type=jnp.float32
    ).astype(jnp.bfloat16)
    columns = lax.dynamic_slice_in_dim(some, lax.axis_index("fsdp") * own_rows, own_rows, 1)

    def in_token_order(whole):
        whole = whole.reshape(n_copy, n_shard * share, -1)
        width = whole.shape[2]

        def swapped(rows, count):
            rows = rows.reshape(n_copy, n_shard, count, width).transpose(1, 0, 2, 3)
            return rows.reshape(n_shard, n_copy * count, width)

        pieces = [
            swapped(whole[:, : n_shard * tall], tall),
            swapped(whole[:, n_shard * tall :], short),
        ]
        return jnp.concatenate(pieces, axis=1).reshape(n_shard * own_tokens, width)

    gram, columns, rounded = lax.optimization_barrier(
        (gram, columns, master.astype(jnp.bfloat16))
    )
    gram_all = lax.all_gather(gram, "dp", axis=0, tiled=True)
    weights = gather_rows(rounded, 1)

    def gathered(pre, call):
        dpre = (cot * slope_of(pre)).astype(jnp.bfloat16)
        return dpre, gather_rows(dpre, call)

    pre = jnp.dot(normed, weights, preferred_element_type=jnp.float32)
    dpre, dpre_all = gathered(pre, 2)
    columns, gram_all, dpre_all = lax.optimization_barrier((columns, gram_all, dpre_all))
    columns_all = lax.all_gather(columns, "dp", axis=0, tiled=True)
    gram_all = lax.optimization_barrier(in_token_order(gram_all))
    shift = lax.dot_general(gram_all, dpre_all, along_rows, preferred_element_type=jnp.float32)
    products = (dpre.astype(jnp.float32) * shift).reshape(-1, 8, 128)
    partial = summed_over("fsdp", jnp.sum(products, axis=(0, 1)).reshape(1, 128), 4)
    squares = jnp.sum(summed_over("dp", partial, 5))
    scale = math.sqrt(FF) / 4.0 / (jnp.sqrt(jnp.maximum(squares, 0.0)) + 1e-12)
    unused, dpre_two = gathered(pre + scale * shift, 3)
    columns_all = lax.optimization_barrier(in_token_order(columns_all))
    second = lax.dot_general(columns_all, dpre_two, along_rows, preferred_element_type=jnp.float32)
    new_momentum = 0.9 * momentum + second
    new_master = master - 0.002 * new_momentum
    return (new_master, new_momentum)


def solution(mesh):
    in_specs = (P("fsdp", None), P("fsdp", "dp"), P(), P("fsdp", "dp"), P("fsdp", "dp"))
    out_specs = (P("fsdp", "dp"), P("fsdp", "dp"))
    return jax.shard_map(local, mesh=mesh, in_specs=in_specs, out_specs=out_specs, check_vma=False)
```

```python
import functools
import math

import jax
import jax.numpy as jnp
from jax import lax
from jax.experimental import pallas as pl
from jax.experimental.pallas import tpu as pltpu
from jax.sharding import PartitionSpec as P

FF = 12288


inv_root_two = 1.0 / math.sqrt(2.0)
inv_root_two_pi = 1.0 / math.sqrt(2.0 * math.pi)


def norm_rows(tokens, gain):
    values = tokens.astype(jnp.float32)
    meansq = jnp.mean(values * values, axis=1, keepdims=True)
    return (values * lax.rsqrt(meansq + 1e-06) * gain).astype(jnp.bfloat16)


def slope_of(pre):
    cdf = 0.5 * (1.0 + jax.scipy.special.erf(pre * inv_root_two))
    return cdf + pre * jnp.exp(-0.5 * pre * pre) * inv_root_two_pi


RING = 8
MESH = pl.DeviceIdType.MESH


def gather_kernel(cut, x_ref, o_ref, side_send, side_recv, ring_send, ring_recv, local_sem):
    me = lax.axis_index("fsdp")
    column = lax.div(me, RING)
    row = lax.rem(me, RING)
    other = 1 - column
    side = other * RING + row
    ring = (
        column * RING + lax.rem(row + 1, RING),
        column * RING + lax.rem(row + RING - 1, RING),
    )
    total = x_ref.shape[0]
    part = (pl.ds(0, cut), pl.ds(cut, total - cut))

    barrier = pltpu.get_barrier_semaphore()
    for peer in (side, ring[0], ring[1]):
        pl.semaphore_signal(barrier, inc=1, device_id={"fsdp": peer}, device_id_type=MESH)
    pl.semaphore_wait(barrier, 3)

    own = pltpu.make_async_copy(x_ref, o_ref.at[me], local_sem)
    own.start()

    started = []

    def move(src, dst, send, recv, peer):
        return pltpu.make_async_remote_copy(
            src_ref=src,
            dst_ref=dst,
            send_sem=send,
            recv_sem=recv,
            device_id={"fsdp": peer},
            device_id_type=MESH,
        )

    def to_side(slot, origin, half, src=None):
        place = o_ref.at[origin, part[half]]
        copy = move(
            place if src is None else src, place, side_send.at[slot], side_recv.at[slot], side
        )
        copy.start()
        started.append(copy)

    def to_ring(unit, way, hop, origin, half, src=None):
        place = o_ref.at[origin, part[half]]
        at = (unit * 2 + way) * 4 + hop - 1
        copy = move(
            place if src is None else src, place, ring_send.at[at], ring_recv.at[at], ring[way]
        )
        copy.start()
        started.append(copy)

    hops = ((4, 3), (3, 4), (4, 3))
    halves = (0, 1, 1)
    columns = (column, column, other)

    first, second = x_ref.at[part[0]], x_ref.at[part[1]]
    to_side(0, me, 1, second)
    for way in range(2):
        to_ring(1, way, 1, me, 1, second)
    for way in range(2):
        to_ring(0, way, 1, me, 0, first)
    to_side(1, me, 0, first)
    place = o_ref.at[side, part[1]]
    move(place, place, side_send.at[0], side_recv.at[0], side).wait_recv()
    for way in range(2):
        to_ring(2, way, 1, side, 1)
    for hop in range(1, 5):
        for unit in (1, 0, 2):
            for way in range(2):
                if hop > hops[unit][way]:
                    continue
                source = lax.rem(row + (RING - hop if way == 0 else hop), RING)
                origin = columns[unit] * RING + source
                place = o_ref.at[origin, part[halves[unit]]]
                at = (unit * 2 + way) * 4 + hop - 1
                move(place, place, ring_send.at[at], ring_recv.at[at], ring[way]).wait_recv()
                if hop < hops[unit][way]:
                    to_ring(unit, way, hop + 1, origin, halves[unit])
                if unit == 0:
                    to_side(2 + way * 4 + hop - 1, origin, 0)
    place = o_ref.at[side, part[0]]
    move(place, place, side_send.at[1], side_recv.at[1], side).wait_recv()
    for way in range(2):
        for hop in range(1, hops[0][way] + 1):
            source = lax.rem(row + (RING - hop if way == 0 else hop), RING)
            place = o_ref.at[other * RING + source, part[0]]
            slot = 2 + way * 4 + hop - 1
            move(place, place, side_send.at[slot], side_recv.at[slot], side).wait_recv()
    for copy in started:
        copy.wait_send()
    own.wait()


def gather_rows(block, call):
    total, width = block.shape
    n_shard = lax.axis_size("fsdp")
    whole = pl.pallas_call(
        functools.partial(gather_kernel, total // 32 * 16),
        out_shape=jax.ShapeDtypeStruct((n_shard, total, width), block.dtype),
        in_specs=[pl.BlockSpec(memory_space=pltpu.VMEM)],
        out_specs=pl.BlockSpec(memory_space=pltpu.VMEM),
        scratch_shapes=[
            pltpu.SemaphoreType.DMA((10,)),
            pltpu.SemaphoreType.DMA((10,)),
            pltpu.SemaphoreType.DMA((24,)),
            pltpu.SemaphoreType.DMA((24,)),
            pltpu.SemaphoreType.DMA,
        ],
        compiler_params=pltpu.CompilerParams(collective_id=call, has_side_effects=True),
        cost_estimate=pl.CostEstimate(
            flops=0, bytes_accessed=30 * n_shard * total * width, transcendentals=0
        ),
    )(block)
    return whole.reshape(n_shard * total, width)


def share_kernel(axis, count, x_ref, o_ref, slots, send, recv):
    me = lax.axis_index(axis)
    peers = [lax.rem(me + step, count) for step in range(1, count)]
    barrier = pltpu.get_barrier_semaphore()
    for peer in peers:
        pl.semaphore_signal(barrier, inc=1, device_id={axis: peer}, device_id_type=MESH)
    pl.semaphore_wait(barrier, count - 1)
    copies = []
    for at, peer in enumerate(peers):
        copy = pltpu.make_async_remote_copy(
            src_ref=x_ref,
            dst_ref=slots.at[at],
            send_sem=send.at[at],
            recv_sem=recv.at[at],
            device_id={axis: peer},
            device_id_type=MESH,
        )
        copy.start()
        copies.append(copy)
    for copy in copies:
        copy.wait()
    o_ref[...] = x_ref[...] + jnp.sum(slots[...], axis=0)


def summed_over(axis, tile, call):
    count = lax.axis_size(axis)
    return pl.pallas_call(
        functools.partial(share_kernel, axis, count),
        out_shape=jax.ShapeDtypeStruct(tile.shape, tile.dtype),
        in_specs=[pl.BlockSpec(memory_space=pltpu.VMEM)],
        out_specs=pl.BlockSpec(memory_space=pltpu.VMEM),
        scratch_shapes=[
            pltpu.VMEM((count - 1,) + tile.shape, tile.dtype),
            pltpu.SemaphoreType.DMA((count - 1,)),
            pltpu.SemaphoreType.DMA((count - 1,)),
        ],
        compiler_params=pltpu.CompilerParams(collective_id=call, has_side_effects=True),
    )(tile)


def local(tokens, cotangent, gain, master, momentum):
    own_rows = master.shape[0]
    own_tokens = tokens.shape[0]
    n_shard = lax.axis_size("fsdp")
    n_copy = lax.axis_size("dp")
    share = own_tokens // n_copy
    along_rows = (((0,), (0,)), ((), ()))
    along_features = (((1,), (1,)), ((), ()))
    cot = cotangent.astype(jnp.float32)

    normed = norm_rows(tokens, gain)
    tall = share // 8 * 8
    short = share - tall
    position = lax.axis_index("dp")
    mine = jnp.concatenate(
        [
            lax.dynamic_slice_in_dim(normed, position * tall, tall, 0),
            lax.dynamic_slice_in_dim(normed, n_copy * tall + position * short, short, 0),
        ]
    )
    some = gather_rows(mine.reshape(-1, 128), 0).reshape(n_shard, share, -1)
    some = jnp.concatenate(
        [
            some[:, :tall].reshape(n_shard * tall, -1),
            some[:, tall:].reshape(n_shard * short, -1),
        ]
    )
    gram = lax.dot_general(
        some, normed, along_features, preferred_element_type=jnp.float32
    ).astype(jnp.bfloat16)
    columns = lax.dynamic_slice_in_dim(some, lax.axis_index("fsdp") * own_rows, own_rows, 1)

    def in_token_order(whole):
        whole = whole.reshape(n_copy, n_shard * share, -1)
        width = whole.shape[2]

        def swapped(rows, count):
            rows = rows.reshape(n_copy, n_shard, count, width).transpose(1, 0, 2, 3)
            return rows.reshape(n_shard, n_copy * count, width)

        pieces = [
            swapped(whole[:, : n_shard * tall], tall),
            swapped(whole[:, n_shard * tall :], short),
        ]
        return jnp.concatenate(pieces, axis=1).reshape(n_shard * own_tokens, width)

    piece, rounded = lax.optimization_barrier(
        (jnp.concatenate([gram, columns], axis=1), master.astype(jnp.bfloat16))
    )
    both = lax.all_gather(piece, "dp", axis=0, tiled=True)
    weights = gather_rows(rounded, 1)

    def gathered(pre, call):
        dpre = (cot * slope_of(pre)).astype(jnp.bfloat16)
        return dpre, gather_rows(dpre, call)

    pre = jnp.dot(normed, weights, preferred_element_type=jnp.float32)
    dpre, dpre_all = gathered(pre, 2)
    gram_all = lax.optimization_barrier(in_token_order(both[:, :own_tokens]))
    shift = lax.dot_general(gram_all, dpre_all, along_rows, preferred_element_type=jnp.float32)
    products = (dpre.astype(jnp.float32) * shift).reshape(-1, 8, 128)
    partial = summed_over("fsdp", jnp.sum(products, axis=(0, 1)).reshape(1, 128), 4)
    squares = jnp.sum(summed_over("dp", partial, 5))
    scale = math.sqrt(FF) / 4.0 / (jnp.sqrt(jnp.maximum(squares, 0.0)) + 1e-12)
    unused, dpre_two = gathered(pre + scale * shift, 3)
    columns_all = lax.optimization_barrier(in_token_order(both[:, own_tokens:]))
    second = lax.dot_general(columns_all, dpre_two, along_rows, preferred_element_type=jnp.float32)
    new_momentum = 0.9 * momentum + second
    new_master = master - 0.002 * new_momentum
    return (new_master, new_momentum)


def solution(mesh):
    in_specs = (P("fsdp", None), P("fsdp", "dp"), P(), P("fsdp", "dp"), P("fsdp", "dp"))
    out_specs = (P("fsdp", "dp"), P("fsdp", "dp"))
    return jax.shard_map(local, mesh=mesh, in_specs=in_specs, out_specs=out_specs, check_vma=False)
```
